32 devices in a mesh: gx: 2 (over x), gy: 4 (over y, core), gz: 4 (over z).
Axes of the slice: x: 2, y: 2, z: 4, core: 2. Of those that a mesh axis runs over, the one named last changes fastest.
Arguments:
- seed_cotangent: bfloat16 [2, 4, 4, 112, 2048], P('gx', 'gy', 'gz'), may hold values from -6 to 6
- trace_operator: bfloat16 [2, 4, 4, 2048, 2048], P('gx', 'gy', 'gz'), may hold values from -0.125 to 0.125
- face_matrices: bfloat16 [2, 4, 4, 6, 340, 340], P('gx', 'gy', 'gz'), may hold values from -0.3125 to 0.3125
- saved_traces: bfloat16 [2, 4, 4, 3, 112, 2048], P('gx', 'gy', 'gz'), may hold values from -6 to 6
- edge_flags: int32 [2, 4, 4, 6], P('gx', 'gy', 'gz'), may hold values 0 or 1
- node_map: int32 [2, 4, 4, 6, 340], P('gx', 'gy', 'gz'), may hold values from 0 to 339, each once within a row
Outputs:
- adjoint_traces: bfloat16 [2, 4, 4, 112, 2048], P('gx', 'gy', 'gz')
- face_gradient: bfloat16 [2, 4, 4, 6, 340, 340], P('gx', 'gy', 'gz')
The draws below stay inside these ranges and needn't reach their ends.
Inputs may be any that keep to these rules, and one draw needn't show every extreme that they name: Each row node_map[.., k, :] names every face node once.
All inputs are finite; a program needn't handle non-finite values. No bound on the sum of `edge_flags` on one device may be relied on, other than what follows from the above.
Results may differ from the reference program's by a relative error of at most 0.0085.
Values may be sent and summed in bfloat16 or wider, within the bound.
A program may use at most 64 MiB of HBM per device.

```python
import jax
import jax.numpy as jnp
from jax import lax

TRACE = 2048
F = 340
COLS = 112
ITERS = 3
NX = 2
NY = 4
NZ = 4


def set_ends(result, own_key, low, top_value):
    longest = result.shape.index(max(result.shape))
    spots = []
    for shift in (0, 1):
        where = [jax.random.randint(jax.random.fold_in(own_key, axis), (), 0, length) for axis, length in enumerate(result.shape)]
        where[longest] = (where[longest] + shift) % result.shape[longest]
        spots.append(tuple(where))
    return result.at[spots[0]].set(low).at[spots[1]].set(top_value)


def level_of(key, shape, split, smallest, largest):
    factor_of = 1.0
    for dim, blocks in split:
        draws = jax.random.uniform(jax.random.fold_in(jax.random.fold_in(key, 6), dim), (blocks,), jnp.float32, smallest / len(split), largest / len(split))
        factor_of = factor_of * jnp.repeat(jnp.exp(draws), shape[dim] // blocks).reshape((-1,) + (1,) * (len(shape) - 1 - dim))
    return factor_of


def scatter_about(rng, dims, deviation, bound, cuts=(), kind=jnp.bfloat16):
    level = level_of(rng, dims, cuts, -0.22, 0.18) if cuts else 1.0
    result = jax.random.normal(rng, dims, jnp.float32) * deviation * level
    return jnp.minimum(jnp.maximum(result, -bound), bound).astype(kind)


def setup_inputs(seed: int = 0) -> dict:
    seeds = jax.random.split(jax.random.key(seed), 7)
    return {
        "seed_cotangent": scatter_about(seeds[0], (NX, NY, NZ, COLS, TRACE), 1.0, 6.0, ((0, 2), (1, 4), (2, 4))),
        "trace_operator": scatter_about(seeds[1], (NX, NY, NZ, TRACE, TRACE), TRACE ** -0.5, 0.125, ((0, 2), (1, 4), (2, 4))),
        "face_matrices": scatter_about(seeds[2], (NX, NY, NZ, 6, F, F), F ** -0.5, 0.3125, ((0, 2), (1, 4), (2, 4))),
        "saved_traces": scatter_about(seeds[3], (NX, NY, NZ, ITERS, COLS, TRACE), 1.0, 6.0, ((0, 2), (1, 4), (2, 4))),
        "edge_flags": set_ends((jax.random.randint(seeds[4], (NX, NY, NZ, 6), 0, 4) < 1).astype(jnp.int32), jax.random.fold_in(seeds[4], 1), 0, 1),
        "node_map": jax.vmap(lambda own: jax.random.permutation(own, F))(jax.random.split(seeds[5], NX * NY * NZ * 6)).reshape((NX, NY, NZ, 6, F)).astype(jnp.int32),
    }


def from_lower(array, axis):
    count = array.shape[axis]
    kept = lax.slice_in_dim(array, 0, count - 1, axis=axis)
    zeros = jnp.zeros_like(lax.slice_in_dim(array, 0, 1, axis=axis))
    return jnp.concatenate([zeros, kept], axis=axis)

def from_upper(array, axis):
    count = array.shape[axis]
    kept = lax.slice_in_dim(array, 1, count, axis=axis)
    zeros = jnp.zeros_like(lax.slice_in_dim(array, 0, 1, axis=axis))
    return jnp.concatenate([kept, zeros], axis=axis)

def local_products(lowered, operator):
    shape = lowered.shape
    flat_rows = lowered.reshape((-1,) + shape[3:])
    flat_ops = operator.reshape((-1,) + operator.shape[3:])

    def single(pieces):
        return jnp.dot(pieces[0], pieces[1], preferred_element_type=jnp.float32).astype(jnp.bfloat16)
    return lax.map(single, (flat_rows, flat_ops)).reshape(shape)

def reference(seed_cotangent, trace_operator, face_matrices, saved_traces, edge_flags, node_map):
    width = face_matrices.shape[-1]
    span = 6 * width
    sweeps = saved_traces.shape[3]
    columns = seed_cotangent.shape[3]
    seeded = seed_cotangent.astype(jnp.float32)
    state = seeded
    total = jnp.zeros(face_matrices.shape, jnp.float32)
    for sweep in range(sweeps):
        hidden = local_products(state.astype(jnp.bfloat16), trace_operator)
        own = jnp.stack([hidden[..., number * width:(number + 1) * width] for number in range(6)], axis=3)
        received = jnp.stack([from_lower(own[:, :, :, 1], 0), from_upper(own[:, :, :, 0], 0), from_lower(own[:, :, :, 3], 1), from_upper(own[:, :, :, 2], 1), from_lower(own[:, :, :, 5], 2), from_upper(own[:, :, :, 4], 2)], axis=3)
        mapped = jnp.take_along_axis(received, node_map[:, :, :, :, None, :], axis=5)
        chosen = jnp.where(edge_flags[..., None, None] == 1, own, mapped)
        fresh = jnp.einsum('xyzkcf,xyzkfg->xyzkcg', chosen.astype(jnp.float32), face_matrices.astype(jnp.float32))
        state = jnp.concatenate([fresh[:, :, :, number] for number in range(6)] + [hidden[..., span:].astype(jnp.float32)], axis=-1) + seeded
        stored = saved_traces[:, :, :, sweeps - 1 - sweep]
        stored_faces = jnp.stack([stored[..., number * width:(number + 1) * width] for number in range(6)], axis=3)
        total = total + jnp.einsum('xyzkcf,xyzkcg->xyzkfg', chosen.astype(jnp.float32), stored_faces.astype(jnp.float32))
    adjoint_traces = state.astype(jnp.bfloat16)
    face_gradient = (total * (1.0 / jnp.sqrt(jnp.float32(columns)))).astype(jnp.bfloat16)
    return (adjoint_traces, face_gradient)
```

```python
import functools
import math

import jax
import jax.numpy as jnp
from jax import lax
from jax.experimental import pallas as pl
from jax.experimental.pallas import tpu as pltpu
from jax.sharding import PartitionSpec as P

LANES = 128
BLOCK = 256
AXES = ("gx", "gy", "gz")


def up(value, step):
    return -(-value // step) * step


def kernel(
    width, seed_hbm, op_hbm, m_hbm, saved_hbm, map_ref, flag_ref, out_hbm, grad_hbm,
    seed_v, op_v, m_v, saved_v, map_v, sel_v, w_v, send_v, recv_v, inp_v, mapped_v, packed_v,
    hid_v, acc_v, st_v, stb_v, g_v, out_v, gout_v,
    in_sem, out_sem, send_sem, recv_sem,
):
    columns, trace = seed_v.shape
    sweeps = saved_v.shape[0]
    pad = up(width, LANES)
    span = 6 * width
    scale = 1.0 / math.sqrt(columns)
    x_end = up(2 * width, BLOCK)
    z_start = (4 * width) // BLOCK * BLOCK
    chunks = ((z_start, trace), (0, x_end), (x_end, z_start))
    order = ((4, 5), (0, 1), (2, 3))

    where = [lax.axis_index(name) for name in AXES]
    has = []
    for axis, name in enumerate(AXES):
        has.append(where[axis] > 0)
        has.append(where[axis] < lax.axis_size(name) - 1)

    def peer(face):
        return {AXES[face // 2]: where[face // 2] + (1 if face % 2 else -1)}

    def span_of(face):
        base = face * width // LANES * LANES
        shift = face * width - base
        return base, shift, up(shift + width, LANES)

    barrier = pltpu.get_barrier_semaphore()
    count = 0
    for face in range(6):
        @pl.when(has[face])
        def _(face=face):
            pl.semaphore_signal(
                barrier, inc=1, device_id=peer(face), device_id_type=pl.DeviceIdType.MESH
            )
        count = count + has[face].astype(jnp.int32)

    seed_in = pltpu.make_async_copy(seed_hbm, seed_v, in_sem.at[0])
    seed_in.start()
    op_in = []
    for number, (start, stop) in enumerate(chunks):
        copy = pltpu.make_async_copy(
            op_hbm.at[:, start:stop], op_v.at[:, start:stop], in_sem.at[1 + number]
        )
        copy.start()
        op_in.append(copy)
    m_in = pltpu.make_async_copy(m_hbm, m_v, in_sem.at[4])
    m_in.start()
    saved_in = pltpu.make_async_copy(saved_hbm, saved_v, in_sem.at[5])
    saved_in.start()

    for face in range(6):
        @pl.when(jnp.logical_not(has[face]))
        def _(face=face):
            for sweep in range(sweeps):
                recv_v[sweep, face] = jnp.zeros((columns, pad), jnp.bfloat16)

    map_v[...] = jnp.full(map_v.shape, -1, jnp.int32)
    map_v[0:6, 0:width] = map_ref[...]
    rows = lax.broadcasted_iota(jnp.int32, (pad, pad), 0)
    lane = lax.broadcasted_iota(jnp.int32, (1, pad), 1)
    for face in range(6):
        flag = (flag_ref[face] == 1).astype(jnp.int32)
        row = map_v[face : face + 1, :]
        row = jnp.where(lane < width, row + (lane - row) * flag, -1)
        sel_v[face] = jnp.where(rows == row, 1.0, 0.0).astype(jnp.bfloat16)
        w_v[face] = jnp.zeros((pad, pad), jnp.bfloat16)

    def remote(sweep, face):
        return pltpu.make_async_remote_copy(
            src_ref=send_v.at[sweep, face],
            dst_ref=recv_v.at[sweep, face ^ 1],
            send_sem=send_sem.at[sweep, face],
            recv_sem=recv_sem.at[sweep, face ^ 1],
            device_id=peer(face),
            device_id_type=pl.DeviceIdType.MESH,
        )

    def arrival(sweep, face):
        return pltpu.make_async_remote_copy(
            src_ref=send_v.at[sweep, face],
            dst_ref=recv_v.at[sweep, face],
            send_sem=send_sem.at[sweep, face],
            recv_sem=recv_sem.at[sweep, face],
            device_id=peer(face),
            device_id_type=pl.DeviceIdType.MESH,
        )

    def take_face(value, shift):
        if shift:
            value = pltpu.roll(value, value.shape[1] - shift, 1)
        return value[:, :pad].astype(jnp.bfloat16)

    def dot(left, right):
        return jnp.dot(left, right, preferred_element_type=jnp.float32)

    def emit(sweep, number):
        for face in order[number]:
            base, shift, extent = span_of(face)
            send_v[sweep, face] = take_face(hid_v[:, base : base + extent], shift)

            @pl.when(has[face])
            def _(face=face):
                remote(sweep, face).start()

    def absorb(sweep, number):
        for face in order[number]:
            @pl.when(has[face])
            def _(face=face):
                arrival(sweep, face).wait_recv()

            inputs = lax.select(flag_ref[face] == 1, send_v[sweep, face], recv_v[sweep, face])
            inp_v[sweep, face] = inputs
            fresh = dot(inputs, w_v[face])
            base, shift, extent = span_of(face)
            if extent > pad:
                fresh = jnp.concatenate(
                    [fresh, jnp.zeros((columns, extent - pad), jnp.float32)], axis=1
                )
            if shift:
                fresh = pltpu.roll(fresh, shift, 1)
            st_v[:, base : base + extent] += fresh

    def map_inputs(sweep):
        for face in range(6):
            mapped_v[face, sweep * columns : (sweep + 1) * columns, :] = dot(
                inp_v[sweep, face], sel_v[face]
            ).astype(jnp.bfloat16)

    def outer(face, start, stop):
        return lax.dot_general(
            mapped_v[face, start:stop, :],
            packed_v[face, start:stop, :],
            (((0,), (0,)), ((), ())),
            preferred_element_type=jnp.float32,
        )

    seed_in.wait()
    for sweep in range(sweeps):
        last = sweep == sweeps - 1
        for number, (start, stop) in enumerate(chunks):
            if sweep == 0:
                op_in[number].wait()
                hidden = dot(seed_v[...], op_v[:, start:stop])
            else:
                hidden = acc_v[:, start:stop] + dot(stb_v[:, 0:x_end], op_v[0:x_end, start:stop])
            hid_v[:, start:stop] = hidden
            if sweep == 0 and number == 0:
                pl.semaphore_wait(barrier, count)
            emit(sweep, number)

        if sweep == 0:
            m_in.wait()
            for face in range(6):
                w_v[face, :, 0:width] = dot(sel_v[face, :, 0:width], m_v[face]).astype(jnp.bfloat16)
        if sweep == 1:
            saved_in.wait()
            for face in range(6):
                base, shift, extent = span_of(face)
                for step in range(sweeps):
                    packed_v[face, step * columns : (step + 1) * columns, :] = take_face(
                        saved_v[sweeps - 1 - step, :, base : base + extent].astype(jnp.float32), shift
                    )
        if sweep >= 1:
            map_inputs(sweep - 1)
        if last:
            for face in range(6):
                g_v[face] = outer(face, 0, sweep * columns)

        st_v[...] = seed_v[...].astype(jnp.float32)
        tail = hid_v[:, trace - LANES : trace].astype(jnp.bfloat16).astype(jnp.float32)
        place = lax.broadcasted_iota(jnp.int32, (columns, LANES), 1) + (trace - LANES)
        st_v[:, trace - LANES : trace] += jnp.where(place >= span, tail, 0.0)
        for number in (2, 0, 1):
            absorb(sweep, number)
            start, stop = chunks[number]
            if not last:
                stb_v[:, start:stop] = st_v[:, start:stop].astype(jnp.bfloat16)
                if number == 2:
                    acc_v[...] = dot(stb_v[:, start:stop], op_v[start:stop, :])
                elif number == 0:
                    acc_v[...] += dot(stb_v[:, start:stop], op_v[start:stop, :])

    out_v[...] = st_v[...].astype(jnp.bfloat16)
    out_copy = pltpu.make_async_copy(out_v, out_hbm, out_sem.at[6])
    out_copy.start()
    map_inputs(sweeps - 1)
    grad_out = []
    for face in range(6):
        total = g_v[face] + outer(face, (sweeps - 1) * columns, sweeps * columns)
        gout_v[face] = (total * scale).astype(jnp.bfloat16)[0:width, 0:width]
        copy = pltpu.make_async_copy(gout_v.at[face], grad_hbm.at[face], out_sem.at[face])
        copy.start()
        grad_out.append(copy)
    for sweep in range(sweeps):
        for face in range(6):
            @pl.when(has[face])
            def _(face=face, sweep=sweep):
                remote(sweep, face).wait_send()
    out_copy.wait()
    for copy in grad_out:
        copy.wait()


def local(seed_cotangent, trace_operator, face_matrices, saved_traces, edge_flags, node_map):
    seed, operator, matrices, stored, flags, mapping = (
        array.reshape(array.shape[3:])
        for array in (
            seed_cotangent, trace_operator, face_matrices, saved_traces, edge_flags, node_map
        )
    )
    width = matrices.shape[-1]
    sweeps, columns, trace = stored.shape
    pad = up(width, LANES)
    bf16, f32 = jnp.bfloat16, jnp.float32
    anywhere = pl.BlockSpec(memory_space=pl.ANY)
    adjoint, gradient = pl.pallas_call(
        functools.partial(kernel, width),
        out_shape=(
            jax.ShapeDtypeStruct(seed.shape, bf16),
            jax.ShapeDtypeStruct(matrices.shape, bf16),
        ),
        in_specs=[anywhere] * 4
        + [pl.BlockSpec(memory_space=pltpu.VMEM), pl.BlockSpec(memory_space=pltpu.SMEM)],
        out_specs=(anywhere, anywhere),
        scratch_shapes=[
            pltpu.VMEM(seed.shape, bf16),
            pltpu.VMEM(operator.shape, bf16),
            pltpu.VMEM(matrices.shape, bf16),
            pltpu.VMEM(stored.shape, bf16),
            pltpu.VMEM((8, pad), jnp.int32),
            pltpu.VMEM((6, pad, pad), bf16),
            pltpu.VMEM((6, pad, pad), bf16),
            pltpu.VMEM((sweeps, 6, columns, pad), bf16),
            pltpu.VMEM((sweeps, 6, columns, pad), bf16),
            pltpu.VMEM((sweeps, 6, columns, pad), bf16),
            pltpu.VMEM((6, sweeps * columns, pad), bf16),
            pltpu.VMEM((6, sweeps * columns, pad), bf16),
            pltpu.VMEM(seed.shape, f32),
            pltpu.VMEM(seed.shape, f32),
            pltpu.VMEM(seed.shape, f32),
            pltpu.VMEM(seed.shape, bf16),
            pltpu.VMEM((6, pad, pad), f32),
            pltpu.VMEM(seed.shape, bf16),
            pltpu.VMEM(matrices.shape, bf16),
            pltpu.SemaphoreType.DMA((6,)),
            pltpu.SemaphoreType.DMA((7,)),
            pltpu.SemaphoreType.DMA((sweeps, 6)),
            pltpu.SemaphoreType.DMA((sweeps, 6)),
        ],
        compiler_params=pltpu.CompilerParams(
            collective_id=0, has_side_effects=True, vmem_limit_bytes=56 * 1024 * 1024
        ),
    )(seed, operator, matrices, stored, mapping, flags)
    return adjoint[None, None, None], gradient[None, None, None]


def solution(mesh):
    return jax.shard_map(
        local,
        mesh=mesh,
        in_specs=(
            P("gx", "gy", "gz", None, None),
            P("gx", "gy", "gz", None, None),
            P("gx", "gy", "gz", None, None, None),
            P("gx", "gy", "gz", None, None, None),
            P("gx", "gy", "gz", None),
            P("gx", "gy", "gz", None, None),
        ),
        out_specs=(P("gx", "gy", "gz", None, None), P("gx", "gy", "gz", None, None, None)),
        check_vma=False,
    )
```

```python
import functools
import math

import jax
import jax.numpy as jnp
from jax import lax
from jax.experimental import pallas as pl
from jax.experimental.pallas import tpu as pltpu
from jax.sharding import PartitionSpec as P

LANES = 128
BLOCK = 256
AXES = ("gx", "gy", "gz")


def up(value, step):
    return -(-value // step) * step


def kernel(
    width, seed_hbm, op_hbm, m_hbm, saved_hbm, map_hbm, flag_ref, out_ref, grad_ref,
    seed_v, op_v, m_v, saved_v, map_v, sel_v, w_v, send_v, recv_v, inp_v, mapped_v, packed_v,
    hid_v, acc_v, st_v, stb_v, g_v,
    in_sem, send_sem, recv_sem,
):
    columns, trace = seed_v.shape
    sweeps = saved_v.shape[0]
    pad = up(width, LANES)
    span = 6 * width
    scale = 1.0 / math.sqrt(columns)
    x_end = up(2 * width, BLOCK)
    z_start = (4 * width) // BLOCK * BLOCK
    chunks = ((z_start, trace), (0, x_end), (x_end, z_start))
    order = ((4, 5), (0, 1), (2, 3))

    where = [lax.axis_index(name) for name in AXES]
    has = []
    for axis, name in enumerate(AXES):
        has.append(where[axis] > 0)
        has.append(where[axis] < lax.axis_size(name) - 1)

    def peer(face):
        return {AXES[face // 2]: where[face // 2] + (1 if face % 2 else -1)}

    def span_of(face):
        base = face * width // LANES * LANES
        shift = face * width - base
        return base, shift, up(shift + width, LANES)

    barrier = pltpu.get_barrier_semaphore()
    count = 0
    for face in range(6):
        @pl.when(has[face])
        def _(face=face):
            pl.semaphore_signal(
                barrier, inc=1, device_id=peer(face), device_id_type=pl.DeviceIdType.MESH
            )
        count = count + has[face].astype(jnp.int32)

    seed_in = pltpu.make_async_copy(seed_hbm, seed_v, in_sem.at[0])
    seed_in.start()
    op_in = []
    for number, (start, stop) in enumerate(chunks):
        copy = pltpu.make_async_copy(
            op_hbm.at[:, start:stop], op_v.at[:, start:stop], in_sem.at[1 + number]
        )
        copy.start()
        op_in.append(copy)
    map_in = pltpu.make_async_copy(map_hbm, map_v, in_sem.at[6])
    map_in.start()
    m_in = pltpu.make_async_copy(m_hbm, m_v, in_sem.at[4])
    m_in.start()
    saved_in = pltpu.make_async_copy(saved_hbm, saved_v, in_sem.at[5])
    saved_in.start()

    for face in range(6):
        @pl.when(jnp.logical_not(has[face]))
        def _(face=face):
            for sweep in range(sweeps):
                recv_v[sweep, face] = jnp.zeros((columns, pad), jnp.bfloat16)

    def remote(sweep, face):
        return pltpu.make_async_remote_copy(
            src_ref=send_v.at[sweep, face],
            dst_ref=recv_v.at[sweep, face ^ 1],
            send_sem=send_sem.at[sweep, face],
            recv_sem=recv_sem.at[sweep, face ^ 1],
            device_id=peer(face),
            device_id_type=pl.DeviceIdType.MESH,
        )

    def arrival(sweep, face):
        return pltpu.make_async_remote_copy(
            src_ref=send_v.at[sweep, face],
            dst_ref=recv_v.at[sweep, face],
            send_sem=send_sem.at[sweep, face],
            recv_sem=recv_sem.at[sweep, face],
            device_id=peer(face),
            device_id_type=pl.DeviceIdType.MESH,
        )

    def take_face(value, shift):
        if shift:
            value = pltpu.roll(value, value.shape[1] - shift, 1)
        return value[:, :pad].astype(jnp.bfloat16)

    def dot(left, right):
        return jnp.dot(left, right, preferred_element_type=jnp.float32)

    def emit(sweep, number):
        for face in order[number]:
            base, shift, extent = span_of(face)
            send_v[sweep, face] = take_face(hid_v[:, base : base + extent], shift)
        for face in order[number]:
            @pl.when(has[face])
            def _(face=face):
                remote(sweep, face).start()

    def absorb(sweep, number):
        for face in order[number]:
            @pl.when(has[face])
            def _(face=face):
                arrival(sweep, face).wait_recv()

        for face in order[number]:
            inputs = lax.select(flag_ref[face] == 1, send_v[sweep, face], recv_v[sweep, face])
            inp_v[sweep, face] = inputs
            fresh = dot(inputs, w_v[face])
            base, shift, extent = span_of(face)
            if extent > pad:
                fresh = jnp.concatenate(
                    [fresh, jnp.zeros((columns, extent - pad), jnp.float32)], axis=1
                )
            if shift:
                fresh = pltpu.roll(fresh, shift, 1)
            st_v[:, base : base + extent] += fresh

    def map_inputs(sweep, faces=range(6)):
        for face in faces:
            mapped_v[face, sweep * columns : (sweep + 1) * columns, :] = dot(
                inp_v[sweep, face], sel_v[face]
            ).astype(jnp.bfloat16)

    def outer(face, start, stop):
        return lax.dot_general(
            mapped_v[face, start:stop, :],
            packed_v[face, start:stop, :],
            (((0,), (0,)), ((), ())),
            preferred_element_type=jnp.float32,
        )

    seed_in.wait()
    for sweep in range(sweeps):
        last = sweep == sweeps - 1
        for number, (start, stop) in enumerate(chunks):
            if sweep == 0:
                op_in[number].wait()
                hidden = dot(seed_v[...], op_v[:, start:stop])
            else:
                hidden = acc_v[:, start:stop] + dot(stb_v[:, 0:x_end], op_v[0:x_end, start:stop])
            hid_v[:, start:stop] = hidden
            if sweep == 0 and number == 0:
                pl.semaphore_wait(barrier, count)
            emit(sweep, number)

        if sweep == 0:
            map_in.wait()
            rows = lax.broadcasted_iota(jnp.int32, (pad, width), 0).astype(jnp.int16)
            lane = lax.broadcasted_iota(jnp.int32, (1, width), 1)
            for face in range(6):
                flag = (flag_ref[face] == 1).astype(jnp.int32)
                row = map_v[face]
                row = row + (lane - row) * flag
                sel_v[face, :, width:pad] = jnp.zeros((pad, pad - width), jnp.bfloat16)
                sel_v[face, :, 0:width] = jnp.where(
                    rows == row.astype(jnp.int16), jnp.bfloat16(1.0), jnp.bfloat16(0.0)
                )
                w_v[face, :, width:pad] = jnp.zeros((pad, pad - width), jnp.bfloat16)
            m_in.wait()
            for face in range(6):
                w_v[face, :, 0:width] = dot(sel_v[face, :, 0:width], m_v[face]).astype(jnp.bfloat16)
        if sweep == 1:
            saved_in.wait()
            for face in range(6):
                base, shift, extent = span_of(face)
                for step in range(sweeps):
                    packed_v[face, step * columns : (step + 1) * columns, :] = take_face(
                        saved_v[sweeps - 1 - step, :, base : base + extent].astype(jnp.float32), shift
                    )
        if sweep >= 1:
            map_inputs(sweep - 1)
        if last:
            for face in range(6):
                g_v[face] = outer(face, 0, sweep * columns)

        st_v[...] = seed_v[...].astype(jnp.float32)
        tail = hid_v[:, trace - LANES : trace].astype(jnp.bfloat16).astype(jnp.float32)
        place = lax.broadcasted_iota(jnp.int32, (columns, LANES), 1) + (trace - LANES)
        st_v[:, trace - LANES : trace] += jnp.where(place >= span, tail, 0.0)
        for number in (2, 0, 1):
            absorb(sweep, number)
            start, stop = chunks[number]
            if last:
                map_inputs(sweep, order[number])
                for face in order[number]:
                    total = g_v[face] + outer(face, sweep * columns, (sweep + 1) * columns)
                    grad_ref[face] = (total * scale).astype(jnp.bfloat16)[0:width, 0:width]
            else:
                stb_v[:, start:stop] = st_v[:, start:stop].astype(jnp.bfloat16)
                if number == 2:
                    acc_v[...] = dot(stb_v[:, start:stop], op_v[start:stop, :])
                elif number == 0:
                    acc_v[...] += dot(stb_v[:, start:stop], op_v[start:stop, :])

    out_ref[...] = st_v[...].astype(jnp.bfloat16)
    for sweep in range(sweeps):
        for face in range(6):
            @pl.when(has[face])
            def _(face=face, sweep=sweep):
                remote(sweep, face).wait_send()


def local(seed_cotangent, trace_operator, face_matrices, saved_traces, edge_flags, node_map):
    seed, operator, matrices, stored, flags, mapping = (
        array.reshape(array.shape[3:])
        for array in (
            seed_cotangent, trace_operator, face_matrices, saved_traces, edge_flags, node_map
        )
    )
    width = matrices.shape[-1]
    sweeps, columns, trace = stored.shape
    pad = up(width, LANES)
    bf16, f32 = jnp.bfloat16, jnp.float32
    anywhere = pl.BlockSpec(memory_space=pltpu.HBM)
    resident = pl.BlockSpec(memory_space=pltpu.VMEM)
    adjoint, gradient = pl.pallas_call(
        functools.partial(kernel, width),
        out_shape=(
            jax.ShapeDtypeStruct(seed.shape, bf16),
            jax.ShapeDtypeStruct(matrices.shape, bf16),
        ),
        in_specs=[anywhere] * 5
        + [pl.BlockSpec(memory_space=pltpu.SMEM)],
        out_specs=(resident, resident),
        scratch_shapes=[
            pltpu.VMEM(seed.shape, bf16),
            pltpu.VMEM(operator.shape, bf16),
            pltpu.VMEM(matrices.shape, bf16),
            pltpu.VMEM(stored.shape, bf16),
            pltpu.VMEM((6, 1, width), jnp.int32),
            pltpu.VMEM((6, pad, pad), bf16),
            pltpu.VMEM((6, pad, pad), bf16),
            pltpu.VMEM((sweeps, 6, columns, pad), bf16),
            pltpu.VMEM((sweeps, 6, columns, pad), bf16),
            pltpu.VMEM((sweeps, 6, columns, pad), bf16),
            pltpu.VMEM((6, sweeps * columns, pad), bf16),
            pltpu.VMEM((6, sweeps * columns, pad), bf16),
            pltpu.VMEM(seed.shape, f32),
            pltpu.VMEM(seed.shape, f32),
            pltpu.VMEM(seed.shape, f32),
            pltpu.VMEM(seed.shape, bf16),
            pltpu.VMEM((6, pad, pad), f32),
            pltpu.SemaphoreType.DMA((7,)),
            pltpu.SemaphoreType.DMA((sweeps, 6)),
            pltpu.SemaphoreType.DMA((sweeps, 6)),
        ],
        compiler_params=pltpu.CompilerParams(
            collective_id=0, has_side_effects=True, vmem_limit_bytes=40 * 1024 * 1024
        ),
    )(*(pltpu.with_memory_space_constraint(array, pltpu.HBM) for array in (seed, operator, matrices, stored, mapping[:, None, :], flags)))
    return adjoint[None, None, None], gradient[None, None, None]


def solution(mesh):
    return jax.shard_map(
        local,
        mesh=mesh,
        in_specs=(
            P("gx", "gy", "gz", None, None),
            P("gx", "gy", "gz", None, None),
            P("gx", "gy", "gz", None, None, None),
            P("gx", "gy", "gz", None, None, None),
            P("gx", "gy", "gz", None),
            P("gx", "gy", "gz", None, None),
        ),
        out_specs=(P("gx", "gy", "gz", None, None), P("gx", "gy", "gz", None, None, None)),
        check_vma=False,
    )
```

```python
import functools
import math

import jax
import jax.numpy as jnp
from jax import lax
from jax.experimental import pallas as pl
from jax.experimental.pallas import tpu as pltpu
from jax.sharding import PartitionSpec as P

LANES = 128
BLOCK = 256
AXES = ("gx", "gy", "gz")


def up(value, step):
    return -(-value // step) * step


def kernel(
    width, seed_hbm, op_hbm, m_hbm, saved_hbm, map_hbm, flag_ref, out_ref, grad_ref,
    seed_v, op_v, m_v, saved_v, map_v, sel_v, w_v, send_v, recv_v, mapped_v, packed_v,
    hid_v, acc_v, st_v, stb_v, g_v,
    in_sem, send_sem, recv_sem,
):
    columns, trace = seed_v.shape
    sweeps = saved_v.shape[0]
    pad = up(width, LANES)
    span = 6 * width
    scale = 1.0 / math.sqrt(columns)
    x_end = up(2 * width, BLOCK)
    z_start = (4 * width) // BLOCK * BLOCK
    chunks = ((z_start, trace), (0, x_end), (x_end, z_start))
    order = ((4, 5), (0, 1), (2, 3))

    where = [lax.axis_index(name) for name in AXES]
    has = []
    for axis, name in enumerate(AXES):
        has.append(where[axis] > 0)
        has.append(where[axis] < lax.axis_size(name) - 1)

    def peer(face):
        return {AXES[face // 2]: where[face // 2] + (1 if face % 2 else -1)}

    def span_of(face):
        base = face * width // LANES * LANES
        shift = face * width - base
        return base, shift, up(shift + width, LANES)

    barrier = pltpu.get_barrier_semaphore()
    count = 0
    for face in range(6):
        @pl.when(has[face])
        def _(face=face):
            pl.semaphore_signal(
                barrier, inc=1, device_id=peer(face), device_id_type=pl.DeviceIdType.MESH
            )
        count = count + has[face].astype(jnp.int32)

    map_in = pltpu.make_async_copy(map_hbm, map_v, in_sem.at[6])
    map_in.start()
    seed_in = pltpu.make_async_copy(seed_hbm, seed_v, in_sem.at[0])
    seed_in.start()
    op_in = []
    for number, (start, stop) in enumerate(chunks):
        copy = pltpu.make_async_copy(
            op_hbm.at[:, start:stop], op_v.at[:, start:stop], in_sem.at[1 + number]
        )
        copy.start()
        op_in.append(copy)
    m_in = pltpu.make_async_copy(m_hbm, m_v, in_sem.at[4])
    m_in.start()
    saved_in = pltpu.make_async_copy(saved_hbm, saved_v, in_sem.at[5])
    saved_in.start()

    for face in range(6):
        @pl.when(jnp.logical_not(has[face]))
        def _(face=face):
            for sweep in range(sweeps):
                recv_v[sweep, face] = jnp.zeros((columns, pad), jnp.bfloat16)

    def remote(sweep, face):
        return pltpu.make_async_remote_copy(
            src_ref=send_v.at[sweep, face],
            dst_ref=recv_v.at[sweep, face ^ 1],
            send_sem=send_sem.at[sweep, face],
            recv_sem=recv_sem.at[sweep, face ^ 1],
            device_id=peer(face),
            device_id_type=pl.DeviceIdType.MESH,
        )

    def arrival(sweep, face):
        return pltpu.make_async_remote_copy(
            src_ref=send_v.at[sweep, face],
            dst_ref=recv_v.at[sweep, face],
            send_sem=send_sem.at[sweep, face],
            recv_sem=recv_sem.at[sweep, face],
            device_id=peer(face),
            device_id_type=pl.DeviceIdType.MESH,
        )

    def take_face(value, shift):
        if shift:
            value = pltpu.roll(value, value.shape[1] - shift, 1)
        return value[:, :pad].astype(jnp.bfloat16)

    def dot(left, right):
        return jnp.dot(left, right, preferred_element_type=jnp.float32)

    def emit(sweep, number):
        for face in order[number]:
            base, shift, extent = span_of(face)
            send_v[sweep, face] = take_face(hid_v[:, base : base + extent], shift)
        for face in order[number]:
            @pl.when(has[face])
            def _(face=face):
                remote(sweep, face).start()

    def absorb(sweep, number):
        for face in order[number]:
            @pl.when(has[face])
            def _(face=face):
                arrival(sweep, face).wait_recv()

        for face in order[number]:
            inputs = lax.select(flag_ref[face] == 1, send_v[sweep, face], recv_v[sweep, face])
            mapped = dot(inputs, sel_v[face]).astype(jnp.bfloat16)
            mapped_v[face, sweep * columns : (sweep + 1) * columns, :] = mapped
            fresh = dot(mapped, w_v[face])
            base, shift, extent = span_of(face)
            if extent > pad:
                fresh = jnp.concatenate(
                    [fresh, jnp.zeros((columns, extent - pad), jnp.float32)], axis=1
                )
            if shift:
                fresh = pltpu.roll(fresh, shift, 1)
            st_v[:, base : base + extent] += fresh

    def outer(face, start, stop):
        return lax.dot_general(
            mapped_v[face, start:stop, :],
            packed_v[face, start:stop, :],
            (((0,), (0,)), ((), ())),
            preferred_element_type=jnp.float32,
        )

    map_in.wait()
    rows = lax.broadcasted_iota(jnp.int32, (pad, width), 0).astype(jnp.int16)
    lane = lax.broadcasted_iota(jnp.int32, (1, width), 1)
    for face in range(6):
        flag = (flag_ref[face] == 1).astype(jnp.int32)
        row = map_v[face]
        row = row + (lane - row) * flag
        sel_v[face, :, width:pad] = jnp.zeros((pad, pad - width), jnp.bfloat16)
        sel_v[face, :, 0:width] = jnp.where(
            rows == row.astype(jnp.int16), jnp.bfloat16(1.0), jnp.bfloat16(0.0)
        )
        w_v[face] = jnp.zeros((pad, pad), jnp.bfloat16)
    seed_in.wait()
    for sweep in range(sweeps):
        last = sweep == sweeps - 1
        for number, (start, stop) in enumerate(chunks):
            if sweep == 0:
                op_in[number].wait()
                hidden = dot(seed_v[...], op_v[:, start:stop])
            else:
                hidden = acc_v[:, start:stop] + dot(stb_v[:, 0:x_end], op_v[0:x_end, start:stop])
            hid_v[:, start:stop] = hidden
            if sweep == 0 and number == 0:
                pl.semaphore_wait(barrier, count)
            emit(sweep, number)

        if sweep == 0:
            m_in.wait()
            for face in range(6):
                w_v[face, 0:width, 0:width] = m_v[face]
            saved_in.wait()
            for face in range(6):
                base, shift, extent = span_of(face)
                for step in range(sweeps):
                    packed_v[face, step * columns : (step + 1) * columns, :] = take_face(
                        saved_v[sweeps - 1 - step, :, base : base + extent].astype(jnp.float32), shift
                    )
        if last:
            for face in range(6):
                g_v[face] = outer(face, 0, sweep * columns)

        st_v[...] = seed_v[...].astype(jnp.float32)
        tail = hid_v[:, trace - LANES : trace].astype(jnp.bfloat16).astype(jnp.float32)
        place = lax.broadcasted_iota(jnp.int32, (columns, LANES), 1) + (trace - LANES)
        st_v[:, trace - LANES : trace] += jnp.where(place >= span, tail, 0.0)
        for number in (2, 0, 1):
            absorb(sweep, number)
            start, stop = chunks[number]
            if last:
                for face in order[number]:
                    total = g_v[face] + outer(face, sweep * columns, (sweep + 1) * columns)
                    grad_ref[face] = (total * scale).astype(jnp.bfloat16)[0:width, 0:width]
            else:
                stb_v[:, start:stop] = st_v[:, start:stop].astype(jnp.bfloat16)
                if number == 2:
                    acc_v[...] = dot(stb_v[:, start:stop], op_v[start:stop, :])
                elif number == 0:
                    acc_v[...] += dot(stb_v[:, start:stop], op_v[start:stop, :])

    out_ref[...] = st_v[...].astype(jnp.bfloat16)
    for sweep in range(sweeps):
        for face in range(6):
            @pl.when(has[face])
            def _(face=face, sweep=sweep):
                remote(sweep, face).wait_send()


def local(seed_cotangent, trace_operator, face_matrices, saved_traces, edge_flags, node_map):
    seed, operator, matrices, stored, flags, mapping = (
        array.reshape(array.shape[3:])
        for array in (
            seed_cotangent, trace_operator, face_matrices, saved_traces, edge_flags, node_map
        )
    )
    width = matrices.shape[-1]
    sweeps, columns, trace = stored.shape
    pad = up(width, LANES)
    bf16, f32 = jnp.bfloat16, jnp.float32
    anywhere = pl.BlockSpec(memory_space=pltpu.HBM)
    resident = pl.BlockSpec(memory_space=pltpu.VMEM)
    adjoint, gradient = pl.pallas_call(
        functools.partial(kernel, width),
        out_shape=(
            jax.ShapeDtypeStruct(seed.shape, bf16),
            jax.ShapeDtypeStruct(matrices.shape, bf16),
        ),
        in_specs=[anywhere] * 5
        + [pl.BlockSpec(memory_space=pltpu.SMEM)],
        out_specs=(resident, resident),
        scratch_shapes=[
            pltpu.VMEM(seed.shape, bf16),
            pltpu.VMEM(operator.shape, bf16),
            pltpu.VMEM(matrices.shape, bf16),
            pltpu.VMEM(stored.shape, bf16),
            pltpu.VMEM((6, 1, width), jnp.int32),
            pltpu.VMEM((6, pad, pad), bf16),
            pltpu.VMEM((6, pad, pad), bf16),
            pltpu.VMEM((sweeps, 6, columns, pad), bf16),
            pltpu.VMEM((sweeps, 6, columns, pad), bf16),
            pltpu.VMEM((6, sweeps * columns, pad), bf16),
            pltpu.VMEM((6, sweeps * columns, pad), bf16),
            pltpu.VMEM(seed.shape, f32),
            pltpu.VMEM(seed.shape, f32),
            pltpu.VMEM(seed.shape, f32),
            pltpu.VMEM(seed.shape, bf16),
            pltpu.VMEM((6, pad, pad), f32),
            pltpu.SemaphoreType.DMA((7,)),
            pltpu.SemaphoreType.DMA((sweeps, 6)),
            pltpu.SemaphoreType.DMA((sweeps, 6)),
        ],
        compiler_params=pltpu.CompilerParams(
            collective_id=0, has_side_effects=True, vmem_limit_bytes=40 * 1024 * 1024
        ),
    )(*(pltpu.with_memory_space_constraint(array, pltpu.HBM) for array in (seed, operator, matrices, stored, mapping[:, None, :], flags)))
    return adjoint[None, None, None], gradient[None, None, None]


def solution(mesh):
    return jax.shard_map(
        local,
        mesh=mesh,
        in_specs=(
            P("gx", "gy", "gz", None, None),
            P("gx", "gy", "gz", None, None),
            P("gx", "gy", "gz", None, None, None),
            P("gx", "gy", "gz", None, None, None),
            P("gx", "gy", "gz", None),
            P("gx", "gy", "gz", None, None),
        ),
        out_specs=(P("gx", "gy", "gz", None, None), P("gx", "gy", "gz", None, None, None)),
        check_vma=False,
    )
```

```python
import functools
import math

import jax
import jax.numpy as jnp
from jax import lax
from jax.experimental import pallas as pl
from jax.experimental.pallas import tpu as pltpu
from jax.sharding import PartitionSpec as P

LANES = 128
BLOCK = 256
AXES = ("gx", "gy", "gz")


def up(value, step):
    return -(-value // step) * step


def kernel(
    width, seed_hbm, op_hbm, m_hbm, saved_hbm, map_hbm, flag_ref, out_ref, grad_ref,
    seed_v, op_v, m_v, saved_v, map_v, sel_v, w_v, send_v, recv_v, inp_v, mapped_v, packed_v,
    hid_v, acc_v, st_v, stb_v, g_v,
    in_sem, send_sem, recv_sem,
):
    columns, trace = seed_v.shape
    sweeps = saved_v.shape[0]
    pad = up(width, LANES)
    span = 6 * width
    scale = 1.0 / math.sqrt(columns)
    x_end = up(2 * width, BLOCK)
    z_start = (4 * width) // BLOCK * BLOCK
    chunks = ((z_start, trace), (0, x_end), (x_end, z_start))
    order = ((4, 5), (0, 1), (2, 3))

    where = [lax.axis_index(name) for name in AXES]
    has = []
    for axis, name in enumerate(AXES):
        has.append(where[axis] > 0)
        has.append(where[axis] < lax.axis_size(name) - 1)

    def peer(face):
        return {AXES[face // 2]: where[face // 2] + (1 if face % 2 else -1)}

    def span_of(face):
        base = face * width // LANES * LANES
        shift = face * width - base
        return base, shift, up(shift + width, LANES)

    barrier = pltpu.get_barrier_semaphore()
    count = 0
    for face in range(6):
        @pl.when(has[face])
        def _(face=face):
            pl.semaphore_signal(
                barrier, inc=1, device_id=peer(face), device_id_type=pl.DeviceIdType.MESH
            )
        count = count + has[face].astype(jnp.int32)

    map_in = pltpu.make_async_copy(map_hbm, map_v, in_sem.at[6])
    map_in.start()
    seed_in = pltpu.make_async_copy(seed_hbm, seed_v, in_sem.at[0])
    seed_in.start()
    op_in = []
    for number, (start, stop) in enumerate(chunks):
        copy = pltpu.make_async_copy(
            op_hbm.at[:, start:stop], op_v.at[:, start:stop], in_sem.at[1 + number]
        )
        copy.start()
        op_in.append(copy)
    m_in = pltpu.make_async_copy(m_hbm, m_v, in_sem.at[4])
    m_in.start()
    saved_in = pltpu.make_async_copy(saved_hbm, saved_v, in_sem.at[5])
    saved_in.start()

    for face in range(6):
        @pl.when(jnp.logical_not(has[face]))
        def _(face=face):
            for sweep in range(sweeps):
                recv_v[sweep, face] = jnp.zeros((columns, pad), jnp.bfloat16)

    def remote(sweep, face):
        return pltpu.make_async_remote_copy(
            src_ref=send_v.at[sweep, face],
            dst_ref=recv_v.at[sweep, face ^ 1],
            send_sem=send_sem.at[sweep, face],
            recv_sem=recv_sem.at[sweep, face ^ 1],
            device_id=peer(face),
            device_id_type=pl.DeviceIdType.MESH,
        )

    def arrival(sweep, face):
        return pltpu.make_async_remote_copy(
            src_ref=send_v.at[sweep, face],
            dst_ref=recv_v.at[sweep, face],
            send_sem=send_sem.at[sweep, face],
            recv_sem=recv_sem.at[sweep, face],
            device_id=peer(face),
            device_id_type=pl.DeviceIdType.MESH,
        )

    def take_face(value, shift):
        if shift:
            value = pltpu.roll(value, value.shape[1] - shift, 1)
        return value[:, :pad].astype(jnp.bfloat16)

    def dot(left, right):
        return jnp.dot(left, right, preferred_element_type=jnp.float32)

    def emit(sweep, number):
        for face in order[number]:
            base, shift, extent = span_of(face)
            send_v[sweep, face] = take_face(hid_v[:, base : base + extent], shift)
        for face in order[number]:
            @pl.when(has[face])
            def _(face=face):
                remote(sweep, face).start()

    def absorb(sweep, number):
        for face in order[number]:
            @pl.when(has[face])
            def _(face=face):
                arrival(sweep, face).wait_recv()

        for face in order[number]:
            inputs = lax.select(flag_ref[face] == 1, send_v[sweep, face], recv_v[sweep, face])
            inp_v[sweep, face] = inputs
            fresh = dot(inputs, w_v[face])
            base, shift, extent = span_of(face)
            if extent > pad:
                fresh = jnp.concatenate(
                    [fresh, jnp.zeros((columns, extent - pad), jnp.float32)], axis=1
                )
            if shift:
                fresh = pltpu.roll(fresh, shift, 1)
            st_v[:, base : base + extent] += fresh

    def map_inputs(sweep, faces=range(6)):
        for face in faces:
            mapped_v[face, sweep * columns : (sweep + 1) * columns, :] = dot(
                inp_v[sweep, face], sel_v[face]
            ).astype(jnp.bfloat16)

    def outer(face, start, stop):
        return lax.dot_general(
            mapped_v[face, start:stop, :],
            packed_v[face, start:stop, :],
            (((0,), (0,)), ((), ())),
            preferred_element_type=jnp.float32,
        )

    map_in.wait()
    rows = lax.broadcasted_iota(jnp.int32, (pad, width), 0).astype(jnp.int16)
    lane = lax.broadcasted_iota(jnp.int32, (1, width), 1)
    for face in range(6):
        flag = (flag_ref[face] == 1).astype(jnp.int32)
        row = map_v[face]
        row = row + (lane - row) * flag
        sel_v[face, :, width:pad] = jnp.zeros((pad, pad - width), jnp.bfloat16)
        sel_v[face, :, 0:width] = jnp.where(
            rows == row.astype(jnp.int16), jnp.bfloat16(1.0), jnp.bfloat16(0.0)
        )
        w_v[face, :, width:pad] = jnp.zeros((pad, pad - width), jnp.bfloat16)
    seed_in.wait()
    for sweep in range(sweeps):
        last = sweep == sweeps - 1
        for number, (start, stop) in enumerate(chunks):
            if sweep == 0:
                op_in[number].wait()
                hidden = dot(seed_v[...], op_v[:, start:stop])
            else:
                hidden = acc_v[:, start:stop] + dot(stb_v[:, 0:x_end], op_v[0:x_end, start:stop])
            hid_v[:, start:stop] = hidden
            if sweep == 0 and number == 0:
                pl.semaphore_wait(barrier, count)
            emit(sweep, number)

        if sweep == 0:
            m_in.wait()
            for face in range(6):
                w_v[face, :, 0:width] = dot(sel_v[face, :, 0:width], m_v[face]).astype(jnp.bfloat16)
        if sweep == 1:
            saved_in.wait()
            for face in range(6):
                base, shift, extent = span_of(face)
                for step in range(sweeps):
                    packed_v[face, step * columns : (step + 1) * columns, :] = take_face(
                        saved_v[sweeps - 1 - step, :, base : base + extent].astype(jnp.float32), shift
                    )
        if sweep >= 1:
            map_inputs(sweep - 1)
        if last:
            for face in range(6):
                g_v[face] = outer(face, 0, sweep * columns)

        st_v[...] = seed_v[...].astype(jnp.float32)
        tail = hid_v[:, trace - LANES : trace].astype(jnp.bfloat16).astype(jnp.float32)
        place = lax.broadcasted_iota(jnp.int32, (columns, LANES), 1) + (trace - LANES)
        st_v[:, trace - LANES : trace] += jnp.where(place >= span, tail, 0.0)
        for number in (2, 0, 1):
            absorb(sweep, number)
            start, stop = chunks[number]
            if last:
                map_inputs(sweep, order[number])
                for face in order[number]:
                    total = g_v[face] + outer(face, sweep * columns, (sweep + 1) * columns)
                    grad_ref[face] = (total * scale).astype(jnp.bfloat16)[0:width, 0:width]
            else:
                stb_v[:, start:stop] = st_v[:, start:stop].astype(jnp.bfloat16)
                if number == 2:
                    acc_v[...] = dot(stb_v[:, start:stop], op_v[start:stop, :])
                elif number == 0:
                    acc_v[...] += dot(stb_v[:, start:stop], op_v[start:stop, :])

    out_ref[...] = st_v[...].astype(jnp.bfloat16)
    for sweep in range(sweeps):
        for face in range(6):
            @pl.when(has[face])
            def _(face=face, sweep=sweep):
                remote(sweep, face).wait_send()


def local(seed_cotangent, trace_operator, face_matrices, saved_traces, edge_flags, node_map):
    seed, operator, matrices, stored, flags, mapping = (
        array.reshape(array.shape[3:])
        for array in (
            seed_cotangent, trace_operator, face_matrices, saved_traces, edge_flags, node_map
        )
    )
    width = matrices.shape[-1]
    sweeps, columns, trace = stored.shape
    pad = up(width, LANES)
    bf16, f32 = jnp.bfloat16, jnp.float32
    anywhere = pl.BlockSpec(memory_space=pltpu.HBM)
    resident = pl.BlockSpec(memory_space=pltpu.VMEM)
    adjoint, gradient = pl.pallas_call(
        functools.partial(kernel, width),
        out_shape=(
            jax.ShapeDtypeStruct(seed.shape, bf16),
            jax.ShapeDtypeStruct(matrices.shape, bf16),
        ),
        in_specs=[anywhere] * 5
        + [pl.BlockSpec(memory_space=pltpu.SMEM)],
        out_specs=(resident, resident),
        scratch_shapes=[
            pltpu.VMEM(seed.shape, bf16),
            pltpu.VMEM(operator.shape, bf16),
            pltpu.VMEM(matrices.shape, bf16),
            pltpu.VMEM(stored.shape, bf16),
            pltpu.VMEM((6, 1, width), jnp.int32),
            pltpu.VMEM((6, pad, pad), bf16),
            pltpu.VMEM((6, pad, pad), bf16),
            pltpu.VMEM((sweeps, 6, columns, pad), bf16),
            pltpu.VMEM((sweeps, 6, columns, pad), bf16),
            pltpu.VMEM((sweeps, 6, columns, pad), bf16),
            pltpu.VMEM((6, sweeps * columns, pad), bf16),
            pltpu.VMEM((6, sweeps * columns, pad), bf16),
            pltpu.VMEM(seed.shape, f32),
            pltpu.VMEM(seed.shape, f32),
            pltpu.VMEM(seed.shape, f32),
            pltpu.VMEM(seed.shape, bf16),
            pltpu.VMEM((6, pad, pad), f32),
            pltpu.SemaphoreType.DMA((7,)),
            pltpu.SemaphoreType.DMA((sweeps, 6)),
            pltpu.SemaphoreType.DMA((sweeps, 6)),
        ],
        compiler_params=pltpu.CompilerParams(
            collective_id=0, has_side_effects=True, vmem_limit_bytes=40 * 1024 * 1024
        ),
    )(*(pltpu.with_memory_space_constraint(array, pltpu.HBM) for array in (seed, operator, matrices, stored, mapping[:, None, :], flags)))
    return adjoint[None, None, None], gradient[None, None, None]


def solution(mesh):
    return jax.shard_map(
        local,
        mesh=mesh,
        in_specs=(
            P("gx", "gy", "gz", None, None),
            P("gx", "gy", "gz", None, None),
            P("gx", "gy", "gz", None, None, None),
            P("gx", "gy", "gz", None, None, None),
            P("gx", "gy", "gz", None),
            P("gx", "gy", "gz", None, None),
        ),
        out_specs=(P("gx", "gy", "gz", None, None), P("gx", "gy", "gz", None, None, None)),
        check_vma=False,
    )
```
